32 devices in a mesh: fsdp: 4 (over z), ctx: 2 (over x), tp: 4 (over y, core).
Axes of the slice: x: 2, y: 2, z: 4, core: 2. Of those that a mesh axis runs over, the one named last changes fastest.
Arguments:
- tokens: bfloat16 [8, 2048, 1024], P('fsdp', ('ctx', 'tp')), may hold values from -6 to 6
- cotangent: bfloat16 [8, 2048, 1024], P('fsdp', ('ctx', 'tp')), may hold values from -6 to 6
- lengths: int32 [8, 2], P('fsdp'), may hold values from 1 to 1536, 1792 in all within a row
- deal: int32 [8, 2048], P('fsdp'), may hold values from 0 to 2047, as said below
- ln1_gain: bfloat16 [1024], P('fsdp'), may hold values from 0.5 to 1.5
- ln1_bias: bfloat16 [1024], P('fsdp'), may hold values from -1.25 to 1.25
- w_qkv: bfloat16 [1024, 3, 1024], P('fsdp', None, 'tp'), may hold values from -0.1875 to 0.1875
- b_qv: bfloat16 [2, 16, 64], P(None, 'tp', 'fsdp'), may hold values from -3 to 3
- w_out: bfloat16 [1024, 1024], P('tp', 'fsdp'), may hold values from -1.5 to 1.5
- b_out: bfloat16 [1024], P('fsdp'), may hold values from -1.25 to 1.25
- ln2_gain: bfloat16 [1024], P('fsdp'), may hold values from 0.5 to 1.5
- ln2_bias: bfloat16 [1024], P('fsdp'), may hold values from -1.25 to 1.25
- w_fc: bfloat16 [1024, 4096], P('fsdp', 'tp'), may hold values from -0.1875 to 0.1875
- b_fc: bfloat16 [64, 64], P('tp', 'fsdp'), may hold values from -1.25 to 1.25
- w_proj: bfloat16 [4096, 1024], P('tp', 'fsdp'), may hold values from -0.125 to 0.125
- b_proj: bfloat16 [1024], P('fsdp'), may hold values from -1.25 to 1.25
Outputs:
- layer_out: bfloat16 [8, 2048, 1024], P('fsdp', ('ctx', 'tp'))
- grad_tokens: float32 [8, 2048, 1024], P('fsdp', ('ctx', 'tp'))
- grad_ln1_gain: float32 [1024], P('fsdp')
- grad_ln1_bias: float32 [1024], P('fsdp')
- grad_w_qkv: float32 [1024, 3, 1024], P('fsdp', None, 'tp')
- grad_b_qv: float32 [2, 16, 64], P(None, 'tp', 'fsdp')
- grad_w_out: float32 [1024, 1024], P('tp', 'fsdp')
- grad_b_out: float32 [1024], P('fsdp')
- grad_ln2_gain: float32 [1024], P('fsdp')
- grad_ln2_bias: float32 [1024], P('fsdp')
- grad_w_fc: float32 [1024, 4096], P('fsdp', 'tp')
- grad_b_fc: float32 [64, 64], P('tp', 'fsdp')
- grad_w_proj: float32 [4096, 1024], P('tp', 'fsdp')
- grad_b_proj: float32 [1024], P('fsdp')
The draws below stay inside these ranges and needn't reach their ends.
Inputs may be any that keep to these rules, and one draw needn't show every extreme that they name: Each row lists the lengths of its 2 sequences in order; they sum to 1792, the rest of the row being padding. `deal`: each row is a permutation of 0 to 2047 that moves aligned blocks of 64 positions whole.
All inputs are finite; a program needn't handle non-finite values.
Results may differ from the reference program's by a relative error of at most 0.019.
Values may be sent and summed in bfloat16 or wider, within the bound.
No kernel may reach another device: no remote copies, remote signals or barrier semaphores. Data moves between devices by JAX's collectives and lax.ppermute only.
A program may use at most 320 MiB of HBM per device.

```python
import math
import jax
import jax.numpy as jnp
import numpy as np
from jax import lax

D = 1024
H = 16
HD = 64
FF = 4096
ROW = 2048
NSEQ = 2
DEAL = 64
ROWS = 8


def draw_deal(key, part):
    block_count = ROW // DEAL
    row_keys = jax.random.split(key, ROWS)
    orders = jax.vmap(lambda row_key: jax.random.permutation(row_key, block_count))(row_keys)
    within = jnp.arange(DEAL, dtype=jnp.int32)
    placed = orders.astype(jnp.int32)[:, :, None] * DEAL + within[None, None, :]
    return placed.reshape(ROWS, ROW).astype(jnp.int32)


def strengthened(array, rng, source, target, parts, factor):
    def block_of(axis_at):
        return (jnp.arange(array.shape[axis_at]) // (array.shape[axis_at] // parts)).reshape((-1,) + (1,) * (array.ndim - 1 - axis_at))

    near = jax.random.permutation(rng, parts)[block_of(target)]
    second = (block_of(target) + parts // 2) % parts
    return jnp.where((block_of(source) == near) | (block_of(source) == second), factor * array, array)


def levels(own_key, shape, cuts, smallest, largest):
    gain, own = 1.0, jax.random.fold_in(own_key, 6)
    for position, blocks in cuts:
        draws = jnp.exp(jax.random.uniform(jax.random.fold_in(own, position), (blocks,), jnp.float32, smallest / len(cuts), largest / len(cuts)))
        gain = gain * jnp.repeat(draws, shape[position] // blocks).reshape([-1 if axis == position else 1 for axis in range(len(shape))])
    return gain


def split_up(amount, total, most, skew):
    weights = [(1 << 20) // math.isqrt(rank ** skew) + 1 for rank in range(2, amount + 1)]
    surplus, counts = total - most - (amount - 1), [1] * (amount - 1)
    while surplus > 0:
        candidates = [i for i in range(amount - 1) if counts[i] < most]
        whole, budget = sum([weights[i] for i in candidates]), surplus
        for i in candidates:
            extra = min(most - counts[i], max(1, budget * weights[i] // whole), surplus)
            counts[i] = counts[i] + extra
            surplus = surplus - extra
    return np.array([most] + counts)


def ragged(rng, number_of, total, bound, skew):
    if number_of == 2:
        one = jax.random.randint(rng, (), max(1, total - bound), min(bound, total - 1) + 1)
        return jnp.stack([one, total - one])
    sizes = jnp.asarray(split_up(number_of, total, bound, skew), jnp.int32)
    couples = (number_of - 1) // 2
    giver, sink = sizes[1:1 + 2 * couples:2], sizes[2:2 + 2 * couples:2]
    slack = jnp.minimum(giver - 1, bound - sink)
    moved = jax.random.randint(jax.random.fold_in(rng, 1), (couples,), 0, 1 << 20) % (slack + 1)
    sizes = sizes.at[1:1 + 2 * couples:2].set(giver - moved).at[2:2 + 2 * couples:2].set(sink + moved)
    return sizes[jax.random.permutation(jax.random.fold_in(rng, 2), number_of)]


def bell_draw(own_key, extent, width, reach, shards=(), held_as=jnp.bfloat16):
    values = width * jax.random.normal(own_key, extent, jnp.float32)
    if shards:
        values = values * levels(own_key, extent, shards, -0.22, 0.18)
    return jnp.clip(values, -reach, reach).astype(held_as)


def bell_draw_with(stream_key, shape, width, limit, pieces, heavy, kind=jnp.bfloat16):
    array = width * jax.random.normal(stream_key, shape, jnp.float32)
    if pieces:
        array = array * levels(stream_key, shape, pieces, -0.22, 0.18)
    return jnp.clip(strengthened(array, jax.random.fold_in(stream_key, 3), *heavy), -limit, limit).astype(kind)


def setup_inputs(seed: int = 0) -> dict:
    key_list = jax.random.split(jax.random.key(seed), 17)
    tokens = bell_draw(key_list[0], (ROWS, ROW, D), 1.0, 6.0, ((0, 4), (1, 8)))
    cotangent = bell_draw_with(key_list[1], (ROWS, ROW, D), 1.0, 6.0, ((0, 4), (1, 8)), (0, 2, 4, 2.0))
    lengths = jax.vmap(lambda own: ragged(own, NSEQ, ROW - ROW // 8, 3 * ROW // 4, 1))(jax.random.split(key_list[2], ROWS)).reshape((ROWS, NSEQ)).astype(jnp.int32)
    deal = draw_deal(jax.random.fold_in(key_list[16], 71), 0)
    ln1_gain = jnp.clip(1.0 + 0.1 * jax.random.normal(key_list[4], (D,), jnp.float32), 0.5, 1.5).astype(jnp.bfloat16)
    ln1_bias = bell_draw(key_list[5], (D,), 0.2, 1.25, ((0, 4),))
    w_qkv = bell_draw(key_list[6], (D, 3, D), D ** -0.5, 0.1875, ((0, 4), (2, 4)))
    b_qv = bell_draw(key_list[7], (2, H, HD), 0.5, 3.0, ((1, 4), (2, 4)))
    w_out = bell_draw(key_list[8], (D, D), (D // 64) ** -0.5, 1.5, ((0, 4), (1, 4)))
    b_out = bell_draw(key_list[9], (D,), 0.2, 1.25, ((0, 4),))
    ln2_gain = jnp.clip(1.0 + 0.1 * jax.random.normal(key_list[10], (D,), jnp.float32), 0.5, 1.5).astype(jnp.bfloat16)
    ln2_bias = bell_draw(key_list[11], (D,), 0.2, 1.25, ((0, 4),))
    w_fc = bell_draw(key_list[12], (D, FF), D ** -0.5, 0.1875, ((0, 4), (1, 4)))
    b_fc = bell_draw(key_list[13], (FF // 64, 64), 0.2, 1.25, ((0, 4), (1, 4)))
    w_proj = bell_draw(key_list[14], (FF, D), (FF // 2) ** -0.5, 0.125, ((0, 4), (1, 4)))
    b_proj = bell_draw(key_list[15], (D,), 0.2, 1.25, ((0, 4),))
    return dict(tokens=tokens, cotangent=cotangent, lengths=lengths, deal=deal, ln1_gain=ln1_gain, ln1_bias=ln1_bias, w_qkv=w_qkv, b_qv=b_qv, w_out=w_out, b_out=b_out, ln2_gain=ln2_gain, ln2_bias=ln2_bias, w_fc=w_fc, b_fc=b_fc, w_proj=w_proj, b_proj=b_proj)


@jax.custom_vjp
def low(v):
    return lax.optimization_barrier(v.astype(jnp.bfloat16)).astype(jnp.float32)

@jax.custom_vjp
def low_back(v):
    return v

def low_keep(v):
    return (low(v), None)

def low_pass(kept, grad):
    return (grad,)

def back_keep(v):
    return (v, None)

def back_low(kept, grad):
    return (low(grad),)
low.defvjp(low_keep, low_pass)
low_back.defvjp(back_keep, back_low)
EPSILON = 1e-05
NEGATIVE = -1e+30
GELU_SCALE = 0.7978845608028654
GELU_CUBIC = 0.044715

def exact_dot(left_side, right_side):
    return jnp.dot(left_side, right_side, precision=lax.Precision.HIGHEST, preferred_element_type=jnp.float32)

def layer_norm(source, gain_vec, bias_vec):
    center = lax.optimization_barrier(jnp.mean(source, axis=-1, keepdims=True))
    offsets = source - center
    spread = lax.optimization_barrier(jnp.mean(offsets * offsets, axis=-1, keepdims=True))
    return offsets * lax.rsqrt(spread + EPSILON) * gain_vec + bias_vec

def gelu_tanh(source):
    return 0.5 * source * (1.0 + jnp.tanh(GELU_SCALE * (source + GELU_CUBIC * source * source * source)))

def row_layer(token_row, param_set, allowed):
    gain_one, bias_one, qkv_weight, qv_bias, out_weight, out_bias, gain_two, bias_two, fc_weight, fc_bias, proj_weight, proj_bias = param_set
    model_width = qkv_weight.shape[0]
    head_count = qv_bias.shape[1]
    head_size = qv_bias.shape[2]
    scaling = head_size ** (-0.5)
    normed_one = low(layer_norm(token_row, gain_one, bias_one))
    projected = exact_dot(normed_one, qkv_weight.reshape(model_width, 3 * model_width))
    head_bias = qv_bias.reshape(2, model_width)
    query_low = low(low_back(projected[:, :model_width] + head_bias[0]))
    key_low = low(low_back(projected[:, model_width:2 * model_width]))
    value_low = low(low_back(projected[:, 2 * model_width:] + head_bias[1]))

    def to_heads(matrix):
        return matrix.reshape(-1, head_count, head_size).transpose(1, 0, 2)

    def attend(triple):
        query_head, key_head, value_head = triple
        scores = low_back(exact_dot(query_head, key_head.T) * scaling)
        scores = jnp.where(allowed, scores, NEGATIVE)
        row_top = lax.optimization_barrier(jnp.max(scores, axis=-1, keepdims=True))
        shifted = jnp.exp(scores - row_top)
        attention = shifted / lax.optimization_barrier(jnp.sum(shifted, axis=-1, keepdims=True))
        return exact_dot(low(attention), value_head)
    mixed_heads = lax.map(jax.checkpoint(attend), (to_heads(query_low), to_heads(key_low), to_heads(value_low)))
    mixed_low = low(low_back(mixed_heads.transpose(1, 0, 2).reshape(-1, model_width)))
    hidden_one = token_row + low_back(exact_dot(mixed_low, out_weight)) + out_bias
    normed_two = low(layer_norm(hidden_one, gain_two, bias_two))
    before = low_back(exact_dot(normed_two, fc_weight) + fc_bias.reshape(-1))
    act_low = low(gelu_tanh(before))
    return hidden_one + low_back(exact_dot(act_low, proj_weight)) + proj_bias

def reference(tokens, cotangent, lengths, deal, ln1_gain, ln1_bias, w_qkv, b_qv, w_out, b_out, ln2_gain, ln2_bias, w_fc, b_fc, w_proj, b_proj):
    param_set = tuple((param.astype(jnp.float32) for param in (ln1_gain, ln1_bias, w_qkv, b_qv, w_out, b_out, ln2_gain, ln2_bias, w_fc, b_fc, w_proj, b_proj)))
    seq_count = lengths.shape[1]

    def one_row(totals, inputs):
        token_row, cot_row, length_row, deal_row = inputs
        seq_ends = jnp.cumsum(length_row).astype(jnp.int32)
        segment = lax.optimization_barrier(jnp.sum((deal_row[:, None] >= seq_ends[None, :]).astype(jnp.int32), axis=1)).astype(jnp.int32)
        valid = (segment < seq_count).astype(jnp.float32)
        allowed = (segment[:, None] == segment[None, :]) & (deal_row[None, :] <= deal_row[:, None])
        layer_out, pull_back = jax.vjp(lambda token_in, params_in: row_layer(token_in, params_in, allowed), token_row.astype(jnp.float32), param_set)
        token_grad, param_grads = pull_back(cot_row.astype(jnp.float32) * valid[:, None])
        totals = jax.tree.map(jnp.add, totals, param_grads)
        return (totals, (layer_out.astype(jnp.bfloat16), token_grad))
    zero_set = tuple((jnp.zeros(param.shape, jnp.float32) for param in param_set))
    totals, (layer_rows, input_grads) = lax.scan(one_row, zero_set, (tokens, cotangent, lengths, deal))
    return (layer_rows, input_grads, totals[0], totals[1], totals[2], totals[3], totals[4], totals[5], totals[6], totals[7], totals[8], totals[9], totals[10], totals[11])
```

```python
import functools

import jax
import jax.numpy as jnp
from jax import lax
from jax.experimental import pallas as pl
from jax.experimental.pallas import tpu as pltpu
from jax.sharding import PartitionSpec as P

EPSILON = 1e-05
NEGATIVE = -1e30
GELU_SCALE = 0.7978845608028654
GELU_CUBIC = 0.044715
DEAL = 64
f32 = jnp.float32
bf16 = jnp.bfloat16
VM = pl.BlockSpec(memory_space=pltpu.VMEM)
SM = pl.BlockSpec(memory_space=pltpu.SMEM)


def dot(a, b):
    return jnp.dot(a, b, preferred_element_type=f32)


def dot_t(a, b):
    return lax.dot_general(a, b, (((1,), (1,)), ((), ())), preferred_element_type=f32)


def t_dot(a, b):
    return lax.dot_general(a, b, (((0,), (0,)), ((), ())), preferred_element_type=f32)


def tile_bounds(info_ref, tile, q_tile, key_tile, blocks):
    per = q_tile // DEAL
    base = 2 * blocks
    lane = lax.broadcasted_iota(jnp.int32, (1, q_tile), 1)
    end_one, end_two = info_ref[4 * blocks], info_ref[4 * blocks + 1]
    start = jnp.zeros((1, q_tile), jnp.int32)
    for b in range(per):
        start = jnp.where(
            lane // DEAL == b, (info_ref[base + tile * per + b] - b) * DEAL, start
        )
    position = start + lane
    low = jnp.where(position >= end_two, end_two, jnp.where(position >= end_one, end_one, 0))
    first = info_ref[base + tile * per] * DEAL
    last = info_ref[base + tile * per + per - 1] * DEAL + DEAL - 1
    first_low = jnp.where(first >= end_two, end_two, jnp.where(first >= end_one, end_one, 0))
    return position, low, first_low // key_tile, last // key_tile + 1


def block_rows(refs, i):
    per = refs[0].shape[0] // DEAL
    return refs[i // per], slice((i % per) * DEAL, (i % per + 1) * DEAL)


def rows_at(block):
    return pl.ds(pl.multiple_of(block * DEAL, DEAL), DEAL)


def block_diag(src, out_ref, heads, size, q_tile):
    row = lax.broadcasted_iota(jnp.int32, (heads * size, q_tile), 0) // size
    for h in range(heads):
        out_ref[:, h * q_tile : (h + 1) * q_tile] = jnp.where(row == h, src, jnp.zeros_like(src))


def load_sorted(info_ref, kv_refs, width, blocks, ks, vs):
    for i in range(2 * blocks):
        ref, rows = block_rows(kv_refs, i)
        to = rows_at(info_ref[i])
        ks[to, :] = ref[rows, :width]
        vs[to, :] = ref[rows, width:]


def fwd_kernel(parts, heads, size, q_tile, key_tile, *refs):
    info_ref = refs[0]
    q_refs = refs[1 : 1 + parts]
    kv_refs = refs[1 + parts : 1 + 3 * parts]
    out_refs = refs[1 + 3 * parts : 1 + 4 * parts]
    ot_ref, log_ref, ks, vt, vs, qs, qtd, os = refs[1 + 4 * parts :]
    width = heads * size
    qn = qs.shape[0]
    blocks = qn // DEAL
    load_sorted(info_ref, kv_refs, width, blocks, ks, vs)
    for i in range(blocks):
        ref, rows = block_rows(q_refs, i)
        qs[rows_at(info_ref[3 * blocks + i]), :] = ref[rows, :] * bf16(size**-0.5)
    kn = ks.shape[0]
    for t in range(kn // key_tile):
        vt[t] = vs[t * key_tile : (t + 1) * key_tile, :].T
    for t in range(qn // q_tile):
        position, low, k_lo, k_hi = tile_bounds(info_ref, t, q_tile, key_tile, blocks)
        block_diag(qs[t * q_tile : (t + 1) * q_tile, :].T, qtd, heads, size, q_tile)
        sub = lax.broadcasted_iota(jnp.int32, (key_tile, q_tile), 0)

        def body(k, carry):
            rows = pl.ds(pl.multiple_of(k * key_tile, key_tile), key_tile)
            kt = ks[rows, :]
            vtt = vt[k]
            kp = sub + k * key_tile
            ok = (kp <= position) & (kp >= low)
            new = []
            for h in range(heads):
                m, total, acc = carry[h]
                s = dot(kt, qtd[:, h * q_tile : (h + 1) * q_tile])
                s = jnp.where(ok, s, NEGATIVE)
                m_new = jnp.maximum(m, jnp.max(s, axis=0, keepdims=True))
                alpha = jnp.exp(m - m_new)
                p = jnp.exp(s - m_new)
                total = total * alpha + jnp.sum(p, axis=0, keepdims=True)
                acc = acc * alpha + dot(vtt[h * size : (h + 1) * size, :], p.astype(bf16))
                new.append((m_new, total, acc))
            return tuple(new)

        init = tuple(
            (
                jnp.full((1, q_tile), NEGATIVE, f32),
                jnp.zeros((1, q_tile), f32),
                jnp.zeros((size, q_tile), f32),
            )
            for _ in range(heads)
        )
        result = lax.fori_loop(k_lo, k_hi, body, init)
        mixed = jnp.concatenate([acc / total for _, total, acc in result], axis=0)
        cols = slice(t * q_tile, (t + 1) * q_tile)
        ot_ref[:, cols] = mixed
        for h, (m, total, _) in enumerate(result):
            log_ref[h : h + 1, cols] = m + jnp.log(total)
        os[cols, :] = mixed.T.astype(bf16)
    for i in range(blocks):
        ref, rows = block_rows(out_refs, i)
        ref[rows, :] = os[rows_at(info_ref[3 * blocks + i]), :]


def bwd_kernel(parts, heads, size, q_tile, key_tile, *refs):
    info_ref = refs[0]
    q_refs = refs[1 : 1 + parts]
    kv_refs = refs[1 + parts : 1 + 3 * parts]
    g_refs = refs[1 + 3 * parts : 1 + 4 * parts]
    ot_ref, log_ref = refs[1 + 4 * parts : 3 + 4 * parts]
    dq_refs = refs[3 + 4 * parts : 3 + 5 * parts]
    dkv_refs = refs[3 + 5 * parts : 3 + 7 * parts]
    ks, kt_s, vs, qs, gs, qtd, gtd, qd, gd, dk, dv, dqs = refs[3 + 7 * parts :]
    width = heads * size
    qn = qs.shape[0]
    blocks = qn // DEAL
    load_sorted(info_ref, kv_refs, width, blocks, ks, vs)
    for i in range(blocks):
        to = rows_at(info_ref[3 * blocks + i])
        ref, rows = block_rows(q_refs, i)
        qs[to, :] = ref[rows, :] * bf16(size**-0.5)
        ref, rows = block_rows(g_refs, i)
        gs[to, :] = ref[rows, :]
    kn = ks.shape[0]
    for t in range(kn // key_tile):
        kt_s[t] = ks[t * key_tile : (t + 1) * key_tile, :].T
    dk[...] = jnp.zeros_like(dk)
    dv[...] = jnp.zeros_like(dv)
    col = lax.broadcasted_iota(jnp.int32, (q_tile, width), 1) // size
    sub = lax.broadcasted_iota(jnp.int32, (key_tile, q_tile), 0)
    for t in range(qn // q_tile):
        cols = slice(t * q_tile, (t + 1) * q_tile)
        position, low, k_lo, k_hi = tile_bounds(info_ref, t, q_tile, key_tile, blocks)
        qtile = qs[cols, :]
        gtile = gs[cols, :]
        gt = gtile.T
        block_diag(qtile.T, qtd, heads, size, q_tile)
        block_diag(gt, gtd, heads, size, q_tile)
        for h in range(heads):
            hc = slice(h * q_tile, (h + 1) * q_tile)
            qd[hc, :] = jnp.where(col == h, qtile, jnp.zeros_like(qtile))
            gd[hc, :] = jnp.where(col == h, gtile, jnp.zeros_like(gtile))
        prod = gt.astype(f32) * ot_ref[:, cols]
        deltas = [
            jnp.sum(prod[h * size : (h + 1) * size], axis=0, keepdims=True) for h in range(heads)
        ]
        logs = [log_ref[h : h + 1, cols] for h in range(heads)]

        def body(k, carry):
            rows = pl.ds(pl.multiple_of(k * key_tile, key_tile), key_tile)
            kt = ks[rows, :]
            vtile = vs[rows, :]
            ktt = kt_s[k]
            kp = sub + k * key_tile
            ok = (kp <= position) & (kp >= low)
            new, probs, grads = [], [], []
            for h in range(heads):
                hc = slice(h * q_tile, (h + 1) * q_tile)
                s = dot(kt, qtd[:, hc])
                p = jnp.exp(jnp.where(ok, s, NEGATIVE) - logs[h])
                dp = dot(vtile, gtd[:, hc])
                ds = (p * (dp - deltas[h])).astype(bf16)
                new.append(carry[h] + dot(ktt[h * size : (h + 1) * size, :], ds))
                probs.append(p.astype(bf16))
                grads.append(ds)
            dv[rows, :] += dot(jnp.concatenate(probs, axis=1), gd[...])
            dk[rows, :] += dot(jnp.concatenate(grads, axis=1), qd[...])
            return tuple(new)

        result = lax.fori_loop(
            k_lo, k_hi, body, tuple(jnp.zeros((size, q_tile), f32) for _ in range(heads))
        )
        dqs[cols, :] = (jnp.concatenate(result, axis=0).T * (size**-0.5)).astype(bf16)
    for i in range(blocks):
        ref, rows = block_rows(dq_refs, i)
        ref[rows, :] = dqs[rows_at(info_ref[3 * blocks + i]), :]
    for i in range(2 * blocks):
        ref, rows = block_rows(dkv_refs, i)
        at = rows_at(info_ref[i])
        ref[rows, :width] = dk[at, :].astype(bf16)
        ref[rows, width:] = dv[at, :].astype(bf16)


def attn_fwd(info, q, kv, heads, size, q_tile=512, key_tile=512):
    parts = len(q)
    rows, w = q[0].shape
    n = parts * rows
    kn = 2 * n
    outs = pl.pallas_call(
        functools.partial(fwd_kernel, parts, heads, size, q_tile, key_tile),
        out_shape=tuple(jax.ShapeDtypeStruct((rows, w), bf16) for _ in range(parts))
        + (jax.ShapeDtypeStruct((w, n), f32), jax.ShapeDtypeStruct((heads, n), f32)),
        in_specs=[SM] + [VM] * (3 * parts),
        out_specs=(VM,) * (parts + 2),
        scratch_shapes=[
            pltpu.VMEM((kn, w), bf16),
            pltpu.VMEM((kn // key_tile, w, key_tile), bf16),
            pltpu.VMEM((kn, w), bf16),
            pltpu.VMEM((n, w), bf16),
            pltpu.VMEM((w, heads * q_tile), bf16),
            pltpu.VMEM((n, w), bf16),
        ],
        cost_estimate=pl.CostEstimate(
            flops=4 * n * kn * w, bytes_accessed=16 * n * w, transcendentals=n * kn * heads // 2
        ),
        compiler_params=pltpu.CompilerParams(vmem_limit_bytes=40 << 20),
        name="attn_fwd",
    )(info, *q, *kv)
    return outs[:parts], outs[parts], outs[parts + 1]


def attn_bwd(info, q, kv, g, ot, log, heads, size, q_tile=256, key_tile=512):
    parts = len(q)
    rows, w = q[0].shape
    n = parts * rows
    kn = 2 * n
    outs = pl.pallas_call(
        functools.partial(bwd_kernel, parts, heads, size, q_tile, key_tile),
        out_shape=tuple(jax.ShapeDtypeStruct((rows, w), bf16) for _ in range(parts))
        + tuple(jax.ShapeDtypeStruct((rows, 2 * w), bf16) for _ in range(2 * parts)),
        in_specs=[SM] + [VM] * (4 * parts + 2),
        out_specs=(VM,) * (3 * parts),
        scratch_shapes=[
            pltpu.VMEM((kn, w), bf16),
            pltpu.VMEM((kn // key_tile, w, key_tile), bf16),
            pltpu.VMEM((kn, w), bf16),
            pltpu.VMEM((n, w), bf16),
            pltpu.VMEM((n, w), bf16),
            pltpu.VMEM((w, heads * q_tile), bf16),
            pltpu.VMEM((w, heads * q_tile), bf16),
            pltpu.VMEM((heads * q_tile, w), bf16),
            pltpu.VMEM((heads * q_tile, w), bf16),
            pltpu.VMEM((kn, w), f32),
            pltpu.VMEM((kn, w), f32),
            pltpu.VMEM((n, w), bf16),
        ],
        cost_estimate=pl.CostEstimate(
            flops=10 * n * kn * w, bytes_accessed=32 * n * w, transcendentals=n * kn * heads // 2
        ),
        compiler_params=pltpu.CompilerParams(vmem_limit_bytes=50 << 20),
        name="attn_bwd",
    )(info, *q, *kv, *g, ot, log)
    return outs[:parts], outs[parts : 2 * parts], outs[2 * parts :]


def swap(x, axis, mask):
    return lax.ppermute(x, axis, [(i, i ^ mask) for i in range(lax.axis_size(axis))])


def gather_tp(own):
    near = swap(own, "tp", 2)
    first = jnp.concatenate([own, swap(own, "tp", 1)], axis=0)
    second = jnp.concatenate([near, swap(near, "tp", 1)], axis=0)
    return first, second


def scatter_tp(first, second):
    s = first.shape[0] // 2
    away = second[:s] + swap(second[s:].astype(bf16), "tp", 1).astype(f32)
    away = swap(away.astype(bf16), "tp", 2).astype(f32)
    here = first[:s] + swap(first[s:].astype(bf16), "tp", 1).astype(f32)
    return here + away


def norm_stats(source):
    center = jnp.mean(source, axis=-1, keepdims=True)
    offsets = source - center
    spread = jnp.mean(offsets * offsets, axis=-1, keepdims=True)
    inverse = lax.rsqrt(spread + EPSILON)
    return offsets * inverse, inverse


def norm_back(grad, normed, inverse, gain):
    scaled = grad * gain
    return (
        scaled
        - jnp.mean(scaled, axis=-1, keepdims=True)
        - normed * jnp.mean(scaled * normed, axis=-1, keepdims=True)
    ) * inverse


def gelu_and_slope(v):
    t = jnp.tanh(GELU_SCALE * (v + GELU_CUBIC * v * v * v))
    slope = 0.5 * (1.0 + t) + 0.5 * v * (1.0 - t * t) * GELU_SCALE * (
        1.0 + 3.0 * GELU_CUBIC * v * v
    )
    return 0.5 * v * (1.0 + t), slope


def shards(
    tokens,
    cotangent,
    lengths,
    deal,
    ln1_gain,
    ln1_bias,
    w_qkv,
    b_qv,
    w_out,
    b_out,
    ln2_gain,
    ln2_bias,
    w_fc,
    b_fc,
    w_proj,
    b_proj,
):
    micro_count, share, model = tokens.shape
    row_len = deal.shape[1]
    fsdp = lax.axis_size("fsdp")
    tp = lax.axis_size("tp")
    ctx_at = lax.axis_index("ctx")
    tp_at = lax.axis_index("tp")
    fsdp_at = lax.axis_index("fsdp")
    part = model // fsdp
    width = w_qkv.shape[2]
    heads = b_qv.shape[1]
    size = width // heads
    hidden = w_fc.shape[1]

    pieces = [ln1_gain, ln1_bias, b_out, ln2_gain, ln2_bias, b_proj, b_qv.reshape(-1), b_fc.reshape(-1)]
    small = lax.all_gather(jnp.concatenate(pieces), "fsdp", axis=0, tiled=False)
    gain_one, bias_one, out_bias, gain_two, bias_two, proj_bias = (
        small[:, i * part : (i + 1) * part].reshape(1, model).astype(f32) for i in range(6)
    )
    rest = small[:, 6 * part :]
    qv = rest[:, : b_qv.size].reshape(fsdp, 2, heads, size // fsdp)
    qv = qv.transpose(1, 2, 0, 3).reshape(2, 1, width).astype(f32)
    fc_bias = rest[:, b_qv.size :].reshape(fsdp, b_fc.shape[0], b_fc.shape[1])
    fc_bias = fc_bias.transpose(1, 0, 2).reshape(1, hidden).astype(f32)

    def gather(w):
        return lax.all_gather(w, "fsdp", axis=0, tiled=True)

    weight_qkv = gather(w_qkv.reshape(part, 3 * width))
    weight_q, weight_kv = weight_qkv[:, :width], weight_qkv[:, width:]
    weight_out = gather(w_out.T)
    weight_fc = gather(w_fc)
    weight_proj = gather(w_proj.T)

    per = share // DEAL
    table = (deal[:, ::DEAL] // DEAL).reshape(micro_count, 2, tp, per)
    order = tp_at ^ jnp.arange(tp)
    table = jnp.take(table, order, axis=2).reshape(micro_count, 2, tp * per)
    own = jnp.take(table, ctx_at, axis=1)
    other = jnp.take(table, 1 - ctx_at, axis=1)
    blocks = tp * per
    rank = jnp.sum((own[:, None, :] < own[:, :, None]).astype(jnp.int32), axis=2)
    ordered = jnp.sum(
        jnp.where(rank[:, :, None] == jnp.arange(blocks)[None, None], own[:, :, None], 0), axis=1
    )
    ends = jnp.cumsum(lengths, axis=1)
    info = jnp.concatenate([own, other, ordered, rank, ends], axis=1)
    own_slots = (ctx_at * tp + tp_at) * share
    own_positions = lax.dynamic_slice_in_dim(deal, own_slots, share, axis=1)

    states = []
    for r in range(micro_count):
        source = tokens[r].astype(f32)
        one, inverse_one = norm_stats(source)
        normed = gather_tp((one * gain_one + bias_one).astype(bf16))
        kv = [(dot(x, weight_kv) + jnp.concatenate([jnp.zeros_like(qv[1]), qv[1]], 1)).astype(bf16) for x in normed]
        kv_other = [swap(x, "ctx", 1) for x in kv]
        q = [(dot(x, weight_q) + qv[0]).astype(bf16) for x in normed]
        valid = (own_positions[r] < ends[r, -1])[:, None]
        out_grad = jnp.where(valid, cotangent[r], jnp.zeros_like(cotangent[r]))
        out_grads = gather_tp(out_grad)
        mixed, mixed_t, log = attn_fwd(info[r], q, kv + kv_other, heads, size)
        hidden_one = source + scatter_tp(*[dot_t(x, weight_out) for x in mixed]) + out_bias
        two, inverse_two = norm_stats(hidden_one)
        second = gather_tp((two * gain_two + bias_two).astype(bf16))
        before = [dot(x, weight_fc) + fc_bias for x in second]
        act = [gelu_and_slope(x)[0].astype(bf16) for x in before]
        layer_out = hidden_one + scatter_tp(*[dot_t(x, weight_proj) for x in act]) + proj_bias
        out_grad = out_grad.astype(f32)
        before_grad = [
            (dot(g, weight_proj) * gelu_and_slope(x)[1]).astype(bf16)
            for g, x in zip(out_grads, before)
        ]
        second_grad = scatter_tp(*[dot_t(x, weight_fc) for x in before_grad])
        hidden_grad = out_grad + norm_back(second_grad, two, inverse_two, gain_two)
        hidden_grads = gather_tp(hidden_grad.astype(bf16))
        mixed_grad = [dot(x, weight_out).astype(bf16) for x in hidden_grads]
        dq, dkv, dkv_other = attn_bwd(info[r], q, kv + kv_other, mixed_grad, mixed_t, log, heads, size)
        dkv = [
            (x.astype(f32) + swap(y, "ctx", 1).astype(f32)).astype(bf16)
            for x, y in zip(dkv, dkv_other)
        ]
        first_grad = scatter_tp(*[dot_t(x, weight_q) + dot_t(y, weight_kv) for x, y in zip(dq, dkv)])
        token_grad = hidden_grad + norm_back(first_grad, one, inverse_one, gain_one)
        vectors = jnp.concatenate(
            [
                jnp.sum(x, axis=0)
                for x in (
                    first_grad * one,
                    first_grad,
                    hidden_grad,
                    second_grad * two,
                    second_grad,
                    out_grad,
                )
            ]
        )
        shared = jnp.concatenate(
            [
                sum(jnp.sum(x.astype(f32), axis=0) for x in dq),
                sum(jnp.sum(x[:, width:].astype(f32), axis=0) for x in dkv),
                sum(jnp.sum(x.astype(f32), axis=0) for x in before_grad),
            ]
        )
        states.append(
            dict(
                layer_out=layer_out.astype(bf16),
                token_grad=token_grad,
                vectors=vectors,
                shared=shared,
                pairs=dict(
                    proj=list(zip(out_grads, act)),
                    fc=list(zip(second, before_grad)),
                    out=list(zip(hidden_grads, mixed)),
                    q=list(zip(normed, dq)),
                    kv=list(zip(normed, dkv)),
                ),
            )
        )

    def weight_grad(*names):
        whole = jnp.concatenate(
            [
                sum(t_dot(a, b) for s in states for a, b in s["pairs"][name]).astype(bf16)
                for name in names
            ],
            axis=1,
        )
        own_part = lax.psum_scatter(whole, "fsdp", scatter_dimension=0, tiled=True)
        return own_part.astype(f32) + swap(own_part, "ctx", 1).astype(f32)

    grad_proj = weight_grad("proj").T
    grad_fc = weight_grad("fc")
    grad_out = weight_grad("out").T
    grad_qkv = weight_grad("q", "kv").reshape(part, 3, width)

    vectors = lax.psum(sum(s["vectors"] for s in states), ("fsdp", "ctx", "tp"))
    vectors = vectors.reshape(6, fsdp, part)
    vectors = lax.dynamic_index_in_dim(vectors, fsdp_at, axis=1, keepdims=False)
    shared = lax.psum(sum(s["shared"] for s in states), ("fsdp", "ctx"))
    grad_qv = shared[: 2 * width].reshape(2, heads, fsdp, size // fsdp)
    grad_qv = lax.dynamic_index_in_dim(grad_qv, fsdp_at, axis=2, keepdims=False)
    grad_fc_bias = shared[2 * width :].reshape(b_fc.shape[0], fsdp, b_fc.shape[1])
    grad_fc_bias = lax.dynamic_index_in_dim(grad_fc_bias, fsdp_at, axis=1, keepdims=False)
    return (
        jnp.stack([s["layer_out"] for s in states]),
        jnp.stack([s["token_grad"] for s in states]),
        vectors[0],
        vectors[1],
        grad_qkv,
        grad_qv,
        grad_out,
        vectors[2],
        vectors[3],
        vectors[4],
        grad_fc,
        grad_fc_bias,
        grad_proj,
        vectors[5],
    )


def solution(mesh):
    in_specs = (
        P("fsdp", ("ctx", "tp"), None),
        P("fsdp", ("ctx", "tp"), None),
        P("fsdp", None),
        P("fsdp", None),
        P("fsdp"),
        P("fsdp"),
        P("fsdp", None, "tp"),
        P(None, "tp", "fsdp"),
        P("tp", "fsdp"),
        P("fsdp"),
        P("fsdp"),
        P("fsdp"),
        P("fsdp", "tp"),
        P("tp", "fsdp"),
        P("tp", "fsdp"),
        P("fsdp"),
    )
    out_specs = (
        P("fsdp", ("ctx", "tp"), None),
        P("fsdp", ("ctx", "tp"), None),
        P("fsdp"),
        P("fsdp"),
        P("fsdp", None, "tp"),
        P(None, "tp", "fsdp"),
        P("tp", "fsdp"),
        P("fsdp"),
        P("fsdp"),
        P("fsdp"),
        P("fsdp", "tp"),
        P("tp", "fsdp"),
        P("tp", "fsdp"),
        P("fsdp"),
    )
    return jax.shard_map(shards, mesh=mesh, in_specs=in_specs, out_specs=out_specs, check_vma=False)
```
